32 devices in a mesh: slab: 8 (over z, x), snap: 4 (over y, core).
Axes of the slice: x: 2, y: 2, z: 4, core: 2. Of those that a mesh axis runs over, the one named last changes fastest.
Arguments:
- direct: bfloat16 [256, 3, 16, 1024], P('snap', None, 'slab'), may hold values from -6 to 6
- adjoint: bfloat16 [256, 3, 16, 1024], P('snap', None, 'slab'), may hold values from -6 to 6
- viscosity: float32 [16, 1024], P('slab'), may hold values from 0.3 to 3
- energy: float32 [1024], replicated, may hold values from 0.3 to 3
Outputs:
- hankel: float32 [256, 256], P(None, 'snap')
The draws below stay inside these ranges and needn't reach their ends.
All inputs are finite; a program needn't handle non-finite values.
Results may differ from the reference program's by a relative error of at most 0.003.
Values may be sent and summed in bfloat16 or wider, within the bound.
A program may use at most 64 MiB of HBM per device.

```python
import math
import jax
import jax.numpy as jnp
from jax import lax

NY = 32
NZ = 32
NX = 16
SNAPS = 256


def shard_levels(key, shape, split, smallest, high):
    factor_of = 1.0
    for axis_at, blocks in split:
        steps = jax.random.uniform(jax.random.fold_in(jax.random.fold_in(key, 6), axis_at), (blocks,), jnp.float32, smallest / len(split), high / len(split))
        factor_of = factor_of * jnp.repeat(jnp.exp(steps), shape[axis_at] // blocks).reshape((-1,) + (1,) * (len(shape) - 1 - axis_at))
    return factor_of


def noise(stream_key, dims, width, most, cuts=(), kind=jnp.bfloat16):
    loudness = shard_levels(stream_key, dims, cuts, -0.22, 0.18) if cuts else 1.0
    drawn = jax.random.normal(stream_key, dims, jnp.float32) * width * loudness
    return jnp.minimum(jnp.maximum(drawn, -most), most).astype(kind)


def setup_inputs(seed: int = 0) -> dict:
    arg_keys = jax.random.split(jax.random.key(seed), 5)
    direct = noise(arg_keys[0], (SNAPS, 3, NX, NY * NZ), 1.0, 6.0, ((0, 4), (2, 8)))
    adjoint = noise(arg_keys[1], (SNAPS, 3, NX, NY * NZ), 1.0, 6.0, ((0, 4), (2, 8)))
    viscosity = jnp.clip(jnp.exp(math.log(3.0) - 2.3025851 * jax.random.uniform(arg_keys[2], (NX, NY * NZ), jnp.float32) ** shard_levels(arg_keys[2], (NX, NY * NZ), ((0, 8),), -0.2, 0.2)), 0.3, 3.0)
    energy = jnp.clip(jnp.exp(jax.random.uniform(arg_keys[3], (NY * NZ,), jnp.float32, math.log(0.3), math.log(3.0))), 0.3, 3.0)
    return {"direct": direct, "adjoint": adjoint, "viscosity": viscosity, "energy": energy}


def plane_shifts(field, ny, nz):
    cells = ny * nz
    zpos = jnp.arange(cells, dtype=jnp.int32) % nz
    blank = jnp.zeros(field.shape[:-1] + (nz,), jnp.float32)
    y_next = jnp.concatenate([field[..., nz:], blank], axis=-1)
    y_prev = jnp.concatenate([blank, field[..., :-nz]], axis=-1)
    z_next = jnp.where(zpos == nz - 1, jnp.roll(field, nz - 1, axis=-1), jnp.roll(field, -1, axis=-1))
    z_prev = jnp.where(zpos == 0, jnp.roll(field, -(nz - 1), axis=-1), jnp.roll(field, 1, axis=-1))
    return y_next + y_prev + z_next + z_prev - 4.0 * field

def apply_operator(padded, viscosity, energy, ny, nz):
    field = padded.astype(jnp.float32)
    planes = field.shape[-2] - 4
    centre = field[..., 2:2 + planes, :]
    streamwise = (-field[..., 0:planes, :] + 16.0 * field[..., 1:1 + planes, :] - 30.0 * centre + 16.0 * field[..., 3:3 + planes, :] - field[..., 4:4 + planes, :]) / 12.0
    lap = streamwise + plane_shifts(centre, ny, nz)
    return (energy * (viscosity * lap - centre)).astype(jnp.bfloat16)

def reference(direct, adjoint, viscosity, energy):

    def one(snapshot):
        padded = jnp.pad(snapshot, ((0, 0), (2, 2), (0, 0)))
        return apply_operator(padded, viscosity, energy, NY, NZ)
    weighted = lax.map(one, direct)
    count = SNAPS
    flat_w = weighted.reshape(count, -1)
    flat_a = adjoint.reshape(count, -1)
    total = lax.dot_general(flat_a, flat_w, (((1,), (1,)), ((), ())), preferred_element_type=jnp.float32)
    return total / (8.0 * math.sqrt(3.0 * NX * NY * NZ))
```

```python
import functools
import math

import jax
import jax.numpy as jnp
import numpy as np
from jax import lax
from jax.experimental import pallas as pl
from jax.experimental.pallas import tpu as pltpu
from jax.sharding import PartitionSpec as P

NY = 32
NZ = 32
LANES = 128
QUARTERS = 4
HALVES = 2
LAG = 2


def plane_matrix():
    inner = np.zeros((LANES, LANES), np.float32)
    up = np.zeros((LANES, LANES), np.float32)
    down = np.zeros((LANES, LANES), np.float32)
    for lane in range(LANES):
        row, z = divmod(lane, NZ)
        inner[lane, lane] -= 4.0
        inner[row * NZ + (z + 1) % NZ, lane] += 1.0
        inner[row * NZ + (z - 1) % NZ, lane] += 1.0
        if lane + NZ < LANES:
            inner[lane + NZ, lane] += 1.0
        else:
            down[lane + NZ - LANES, lane] += 1.0
        if lane - NZ >= 0:
            inner[lane - NZ, lane] += 1.0
        else:
            up[lane - NZ + LANES, lane] += 1.0
    return np.concatenate([inner, up, down], axis=1)


def kernel(slabs, snaps, reduce_here, scale,
           d_ref, a_ref, v_ref, e_ref, m_ref, out_ref,
           dv, halo, av, at, wt, ab, wb, e16, acc, rs,
           loc_sem, px_s, px_r, pz_s, pz_r, ac_s, ac_r, ay_s, ay_r, af_s, af_r,
           rs_s, rs_r, ag_s, ag_r):
    cols, comps, rows = d_ref.shape[0], d_ref.shape[1], d_ref.shape[2]
    chips = snaps // 2
    i = lax.axis_index("slab")
    n = lax.axis_index("snap")
    parity = i % 2
    pair = i + 1 - 2 * parity
    step = 2 - 4 * parity
    z_to = i + step
    z_from = i - step
    has_to = jnp.logical_and(z_to >= 0, z_to < slabs)
    has_from = jnp.logical_and(z_from >= 0, z_from < slabs)
    chip, core = n // 2, n % 2
    mate = chip * 2 + 1 - core
    pair_slot = 1 - parity
    z_slot = parity
    dq = cols // QUARTERS
    ah = cols // HALVES

    def dev(slab, snap):
        return {"slab": slab, "snap": snap}

    barrier = pltpu.get_barrier_semaphore()

    def greet(slab, snap):
        pl.semaphore_signal(barrier, 1, device_id=dev(slab, snap),
                            device_id_type=pl.DeviceIdType.MESH)

    greet(i, mate)
    for t in range(1, chips):
        greet(i, ((chip + t) % chips) * 2 + core)
    if reduce_here:
        for k in range(1, slabs):
            greet((i + k) % slabs, n)
        pl.semaphore_wait(barrier, chips + slabs - 1)
    else:
        greet(pair, n)

        @pl.when(has_to)
        def _():
            greet(z_to, n)

        @pl.when(has_from)
        def _():
            greet(z_from, n)

        pl.semaphore_wait(
            barrier, chips + 1 + has_to.astype(jnp.int32) + has_from.astype(jnp.int32))

    def remote(src, dst, s, r, slab, snap):
        return pltpu.make_async_remote_copy(
            src_ref=src, dst_ref=dst, send_sem=s, recv_sem=r,
            device_id=dev(slab, snap), device_id_type=pl.DeviceIdType.MESH)

    def px(c, q):
        part = pl.ds(q * dq, dq)
        return remote(d_ref.at[part, c], halo.at[parity, part, c],
                      px_s.at[c, q], px_r.at[c, q], pair, n)

    def pz(c, q):
        part = pl.ds(q * dq, dq)
        return remote(halo.at[pair_slot, part, c], halo.at[z_slot, part, c],
                      pz_s.at[c, q], pz_r.at[c, q], z_to, n)

    def ac(c):
        return remote(a_ref.at[:, c], av.at[n, :, c], ac_s.at[c], ac_r.at[c], i, mate)

    def ay(t, c, h):
        part = pl.ds(h * ah, ah)
        return remote(a_ref.at[part, c], av.at[n, part, c],
                      ay_s.at[t, c, h], ay_r.at[t, c, h], i, ((chip + t) % chips) * 2 + core)

    def af(t, c, h):
        part = pl.ds(h * ah, ah)
        source = ((chip + chips - t) % chips) * 2 + core
        return remote(av.at[source, part, c], av.at[source, part, c],
                      af_s.at[t, c, h], af_r.at[t, c, h], i, mate)

    def local_d(c):
        return pltpu.make_async_copy(d_ref.at[:, c], dv.at[:, c], loc_sem.at[0, c])

    def local_a(c):
        return pltpu.make_async_copy(a_ref.at[:, c], av.at[n, :, c], loc_sem.at[1, c])

    for c in range(comps):
        for q in range(QUARTERS):
            px(c, q).start()
        for h in range(HALVES):
            for t in range(1, chips):
                ay(t, c, h).start()
    for c in range(comps):
        local_d(c).start()
        local_a(c).start()
        ac(c).start()

    for j in range(rows // 2):
        e16[2 * j:2 * j + 2, :] = jnp.broadcast_to(e_ref[j:j + 1, :], (2, LANES))

    @pl.when(jnp.logical_not(has_from))
    def _():
        halo[z_slot] = jnp.zeros(halo.shape[1:], halo.dtype)

    group = 4
    span = group * rows
    row_at = lax.broadcasted_iota(jnp.int32, (span, LANES), 0)
    odd = row_at % 2 == 1
    in_snap = row_at % rows

    def stencil(c, q):
        v = jnp.concatenate([v_ref[...]] * group, axis=0)
        e = jnp.concatenate([e16[...]] * group, axis=0)

        def body(g, carry):
            at_snap = q * dq + g * group
            part = pl.ds(at_snap, group)
            o16 = dv[part, c].reshape(span, LANES)
            lo = halo[0, part, c].reshape(span, LANES).astype(jnp.float32)
            hi = halo[1, part, c].reshape(span, LANES).astype(jnp.float32)
            o = o16.astype(jnp.float32)
            y = jnp.dot(o16, m_ref[...], preferred_element_type=jnp.float32)
            t = o + jnp.where(odd, lo, hi)
            swapped = jnp.where(odd, pltpu.roll(t, 1, 0), pltpu.roll(t, span - 1, 0))
            stream = (16.0 * swapped - 30.0 * o - lo - hi) * (1.0 / 12.0)
            up = pltpu.roll(y[:, LANES:2 * LANES], 2, 0)
            down = pltpu.roll(y[:, 2 * LANES:], span - 2, 0)
            lap = stream + y[:, :LANES]
            lap = lap + jnp.where(in_snap >= 2, up, 0.0)
            lap = lap + jnp.where(in_snap < rows - 2, down, 0.0)
            wt[pl.ds(pl.multiple_of(at_snap * rows, span), span), :] = e * (v * lap - o)
            return carry

        lax.fori_loop(0, dq // group, body, 0)

    def multiply(c):
        def widen(b, carry):
            at[pl.ds(pl.multiple_of(b * cols * rows, cols * rows), cols * rows), :] = (
                av[b, :, c].reshape(cols * rows, LANES).astype(jnp.float32))
            return carry

        lax.fori_loop(0, snaps, widen, 0)
        for r in range(rows):
            ab[:, r * LANES:(r + 1) * LANES] = at[
                pl.ds(r, snaps * cols, stride=rows), :].astype(jnp.bfloat16)
            wb[:, r * LANES:(r + 1) * LANES] = wt[
                pl.ds(r, cols, stride=rows), :].astype(jnp.bfloat16)
        tile = lax.dot_general(wb[...], ab[...], (((1,), (1,)), ((), ())),
                               preferred_element_type=jnp.float32)
        if c == 0:
            acc[...] = tile
        else:
            acc[...] += tile

    def finish(g):
        c, q = divmod(g, QUARTERS)
        if q == 0:
            local_d(c).wait()

        @pl.when(has_from)
        def _():
            pz(c, q).wait_recv()

        stencil(c, q)
        if q == QUARTERS - 1:
            local_a(c).wait()
            ac(c).wait_recv()
            for t in range(1, chips):
                for h in range(HALVES):
                    af(t, c, h).wait_recv()
            multiply(c)

    total = comps * QUARTERS
    per_half = QUARTERS // HALVES
    for g in range(total):
        c, q = divmod(g, QUARTERS)
        px(c, q).wait_recv()

        @pl.when(has_to)
        def _():
            pz(c, q).start()

        if q % per_half == per_half - 1:
            h = q // per_half
            for t in range(1, chips):
                ay(t, c, h).wait_recv()
                af(t, c, h).start()
        if g >= LAG:
            finish(g - LAG)
    for g in range(total - LAG, total):
        finish(g)

    if reduce_here:
        share = cols // slabs

        def rows_of(slab):
            return pl.ds(pl.multiple_of(slab * share, share), share)

        def scatter(k):
            to = (i + k) % slabs
            return remote(acc.at[rows_of(to)], rs.at[k], rs_s.at[k], rs_r.at[k], to, n)

        def gather(k):
            return remote(rs.at[0], out_ref.at[rows_of(i)], ag_s.at[k], ag_r.at[k],
                          (i + k) % slabs, n)

        def gathered(k):
            source = (i + slabs - k) % slabs
            return remote(rs.at[0], out_ref.at[rows_of(source)], ag_s.at[k], ag_r.at[k],
                          (i + k) % slabs, n)

        for k in range(1, slabs):
            scatter(k).start()
        summed = acc[rows_of(i), :]
        for k in range(1, slabs):
            scatter(k).wait_recv()
            summed = summed + rs[k]
        summed = summed * scale
        rs[0] = summed
        for k in range(1, slabs):
            gather(k).start()
        out_ref[rows_of(i), :] = summed
        for k in range(1, slabs):
            gathered(k).wait_recv()
        for k in range(1, slabs):
            scatter(k).wait_send()
            gather(k).wait_send()
    else:
        out_ref[...] = acc[...] * scale

    for c in range(comps):
        ac(c).wait_send()
        for q in range(QUARTERS):
            px(c, q).wait_send()

            @pl.when(has_to)
            def _():
                pz(c, q).wait_send()

        for t in range(1, chips):
            for h in range(HALVES):
                ay(t, c, h).wait_send()
                af(t, c, h).wait_send()


def tiles_first(block):
    lead, (planes, cells) = block.shape[:-2], block.shape[-2:]
    split = block.reshape(lead + (planes, cells // LANES, LANES))
    return jnp.swapaxes(split, -3, -2).reshape(lead + (planes * cells // LANES, LANES))


def per_device(slabs, snaps, direct, adjoint, viscosity, energy):
    cols, comps, planes, cells = direct.shape
    rows = planes * cells // LANES
    scale = 1.0 / (8.0 * math.sqrt(comps * planes * slabs * cells))
    reduce_here = cols % (8 * slabs) == 0
    share = cols // slabs if reduce_here else 8
    halves = (snaps // 2, comps, HALVES)
    quarters = (comps, QUARTERS)
    dma = pltpu.SemaphoreType.DMA
    block = (cols, comps, rows, LANES)
    vmem = pl.BlockSpec(memory_space=pltpu.VMEM)
    hbm = pl.BlockSpec(memory_space=pltpu.HBM)
    out = pl.pallas_call(
        functools.partial(kernel, slabs, snaps, reduce_here, scale),
        out_shape=jax.ShapeDtypeStruct((cols, snaps * cols), jnp.float32),
        in_specs=[hbm, hbm, vmem, vmem, vmem],
        out_specs=vmem,
        scratch_shapes=[
            pltpu.VMEM(block, jnp.bfloat16),
            pltpu.VMEM((2,) + block, jnp.bfloat16),
            pltpu.VMEM((snaps,) + block, jnp.bfloat16),
            pltpu.VMEM((snaps * cols * rows, LANES), jnp.float32),
            pltpu.VMEM((cols * rows, LANES), jnp.float32),
            pltpu.VMEM((snaps * cols, rows * LANES), jnp.bfloat16),
            pltpu.VMEM((cols, rows * LANES), jnp.bfloat16),
            pltpu.VMEM((rows, LANES), jnp.float32),
            pltpu.VMEM((cols, snaps * cols), jnp.float32),
            pltpu.VMEM((max(slabs, 1) if reduce_here else 1, share, snaps * cols), jnp.float32),
            dma((2, comps)),
            dma(quarters), dma(quarters),
            dma(quarters), dma(quarters),
            dma((comps,)), dma((comps,)),
            dma(halves), dma(halves),
            dma(halves), dma(halves),
            dma((slabs,)), dma((slabs,)),
            dma((slabs,)), dma((slabs,)),
        ],
        compiler_params=pltpu.CompilerParams(collective_id=0, has_side_effects=True),
    )(
        tiles_first(direct), tiles_first(adjoint), tiles_first(viscosity),
        energy.reshape(cells // LANES, LANES), jnp.asarray(plane_matrix(), jnp.bfloat16),
    )
    if not reduce_here:
        out = lax.psum(out, "slab")
    return out.T


def solution(mesh):
    placed = (P("snap", None, "slab", None), P("snap", None, "slab", None), P("slab", None), P())
    body = functools.partial(per_device, mesh.shape["slab"], mesh.shape["snap"])
    return jax.shard_map(
        body, mesh=mesh, in_specs=placed, out_specs=P(None, "snap"), check_vma=False
    )
```

```python
import functools
import math

import jax
import jax.numpy as jnp
import numpy as np
from jax import lax
from jax.experimental import pallas as pl
from jax.experimental.pallas import tpu as pltpu
from jax.sharding import PartitionSpec as P

NY = 32
NZ = 32
LANES = 128
QUARTERS = 4
HALVES = 2
LAG = 2
GROUP = 16


def plane_matrix():
    inner = np.zeros((LANES, LANES), np.float32)
    up = np.zeros((LANES, LANES), np.float32)
    down = np.zeros((LANES, LANES), np.float32)
    for lane in range(LANES):
        row, z = divmod(lane, NZ)
        inner[lane, lane] -= 4.0
        inner[row * NZ + (z + 1) % NZ, lane] += 1.0
        inner[row * NZ + (z - 1) % NZ, lane] += 1.0
        if lane + NZ < LANES:
            inner[lane + NZ, lane] += 1.0
        else:
            down[lane + NZ - LANES, lane] += 1.0
        if lane - NZ >= 0:
            inner[lane - NZ, lane] += 1.0
        else:
            up[lane - NZ + LANES, lane] += 1.0
    return np.concatenate([inner, up, down], axis=1)


def kernel(slabs, snaps, reduce_here, scale,
           d_ref, a_ref, v_hbm, e_hbm, m_hbm, out_ref,
           v_ref, e_ref, m_ref, far, dv, halo, av, at, wt, ab, wb, e16, acc, rs,
           loc_sem, px_s, px_r, pz_s, pz_r, ac_s, ac_r, ay_s, ay_r, af_s, af_r,
           rs_s, rs_r, ag_s, ag_r):
    cols, comps, rows = d_ref.shape[0], d_ref.shape[1], d_ref.shape[2]
    chips = snaps // 2
    i = lax.axis_index("slab")
    n = lax.axis_index("snap")
    parity = i % 2
    pair = i + 1 - 2 * parity
    step = 2 - 4 * parity
    z_to = i + step
    z_from = i - step
    has_to = jnp.logical_and(z_to >= 0, z_to < slabs)
    has_from = jnp.logical_and(z_from >= 0, z_from < slabs)
    chip, core = n // 2, n % 2
    mate = chip * 2 + 1 - core
    pair_slot = 1 - parity
    z_slot = parity
    dq = cols // QUARTERS
    per_half = QUARTERS // HALVES
    ah = cols // HALVES

    def dev(slab, snap):
        return {"slab": slab, "snap": snap}

    def remote(src, dst, s, r, slab, snap):
        return pltpu.make_async_remote_copy(
            src_ref=src, dst_ref=dst, send_sem=s, recv_sem=r,
            device_id=dev(slab, snap), device_id_type=pl.DeviceIdType.MESH)

    def px(c, q):
        part = pl.ds(q * dq, dq)
        return remote(d_ref.at[part, c], halo.at[parity, part, c],
                      px_s.at[c, q], px_r.at[c, q], pair, n)

    def pz(c, q):
        part = pl.ds(q * dq, dq)
        return remote(halo.at[pair_slot, part, c], halo.at[z_slot, part, c],
                      pz_s.at[c, q], pz_r.at[c, q], z_to, n)

    def ac(c):
        return remote(a_ref.at[:, c], av.at[n, :, c], ac_s.at[c], ac_r.at[c], i, mate)

    def ay(t, c, h):
        part = pl.ds(h * ah, ah)
        return remote(a_ref.at[part, c], av.at[n, part, c],
                      ay_s.at[t, c, h], ay_r.at[t, c, h], i, ((chip + t) % chips) * 2 + core)

    def af(t, c, h):
        part = pl.ds(h * ah, ah)
        source = ((chip + chips - t) % chips) * 2 + core
        return remote(av.at[source, part, c], av.at[source, part, c],
                      af_s.at[t, c, h], af_r.at[t, c, h], i, mate)

    def local_d(c):
        return pltpu.make_async_copy(d_ref.at[:, c], dv.at[:, c], loc_sem.at[0, c])

    def local_a(c):
        return pltpu.make_async_copy(a_ref.at[:, c], av.at[n, :, c], loc_sem.at[1, c])

    barrier = pltpu.get_barrier_semaphore()

    def greet(slab, snap):
        pl.semaphore_signal(barrier, 1, device_id=dev(slab, snap),
                            device_id_type=pl.DeviceIdType.MESH)

    greet(i, mate)
    for t in range(1, chips):
        greet(i, ((chip + t) % chips) * 2 + core)
    near = 1 + has_to.astype(jnp.int32) + has_from.astype(jnp.int32)

    def tell_near(sem):
        def tell(slab):
            pl.semaphore_signal(sem, 1, device_id=dev(slab, n),
                                device_id_type=pl.DeviceIdType.MESH)

        tell(pair)
        pl.when(has_to)(lambda: tell(z_to))
        pl.when(has_from)(lambda: tell(z_from))

    tell_near(barrier)
    small = [pltpu.make_async_copy(v_hbm, v_ref, loc_sem.at[2, 0]),
             pltpu.make_async_copy(e_hbm, e_ref, loc_sem.at[2, 1]),
             pltpu.make_async_copy(m_hbm, m_ref, loc_sem.at[2, 2])]
    for copy in small:
        copy.start()
    for c in range(comps):
        local_d(c).start()
        local_a(c).start()
    pl.semaphore_wait(barrier, chips + near)

    for c in range(comps):
        for q in range(QUARTERS):
            px(c, q).start()
        for h in range(HALVES):
            for t in range(1, chips):
                ay(t, c, h).start()
    for c in range(comps):
        ac(c).start()
    for copy in small:
        copy.wait()
    for j in range(rows // 2):
        e16[2 * j:2 * j + 2, :] = jnp.broadcast_to(e_ref[j:j + 1, :], (2, LANES))

    @pl.when(jnp.logical_not(has_from))
    def _():
        halo[z_slot] = jnp.zeros(halo.shape[1:], halo.dtype)

    group = GROUP
    span = group * rows
    row_at = lax.broadcasted_iota(jnp.int32, (span, LANES), 0)
    odd = row_at % 2 == 1
    in_snap = row_at % rows

    def stencil(c, q):
        v = jnp.concatenate([v_ref[...]] * group, axis=0)
        e = jnp.concatenate([e16[...]] * group, axis=0)

        def body(g, carry):
            at_snap = q * dq + g * group
            part = pl.ds(at_snap, group)
            o16 = dv[part, c].reshape(span, LANES)
            lo = halo[0, part, c].reshape(span, LANES).astype(jnp.float32)
            hi = halo[1, part, c].reshape(span, LANES).astype(jnp.float32)
            o = o16.astype(jnp.float32)
            y = jnp.dot(o16, m_ref[...], preferred_element_type=jnp.float32)
            t = o + jnp.where(odd, lo, hi)
            swapped = jnp.where(odd, pltpu.roll(t, 1, 0), pltpu.roll(t, span - 1, 0))
            stream = (16.0 * swapped - 30.0 * o - lo - hi) * (1.0 / 12.0)
            up = pltpu.roll(y[:, LANES:2 * LANES], 2, 0)
            down = pltpu.roll(y[:, 2 * LANES:], span - 2, 0)
            lap = stream + y[:, :LANES]
            lap = lap + jnp.where(in_snap >= 2, up, 0.0)
            lap = lap + jnp.where(in_snap < rows - 2, down, 0.0)
            wt[pl.ds(pl.multiple_of(at_snap * rows, span), span), :] = e * (v * lap - o)
            return carry

        lax.fori_loop(0, dq // group, body, 0)

    def widen(b, c, h):
        first = b * cols + h * ah
        at[...] = av[b, pl.ds(h * ah, ah), c].reshape(ah * rows, LANES).astype(jnp.float32)
        for r in range(rows):
            ab[pl.ds(pl.multiple_of(first, ah), ah), r * LANES:(r + 1) * LANES] = at[
                pl.ds(r, ah, stride=rows), :].astype(jnp.bfloat16)

    def widen_chip(chip_at, c, h):
        for b in range(2):
            widen(chip_at * 2 + b, c, h)

    def multiply(c):
        for r in range(rows):
            wb[:, r * LANES:(r + 1) * LANES] = wt[
                pl.ds(r, cols, stride=rows), :].astype(jnp.bfloat16)
        tile = lax.dot_general(wb[...], ab[...], (((1,), (1,)), ((), ())),
                               preferred_element_type=jnp.float32)
        if c == 0:
            acc[...] = tile
        else:
            acc[...] += tile

    def finish(g):
        c, q = divmod(g, QUARTERS)
        if q == 0:
            local_d(c).wait()
        if q % per_half == per_half - 1:
            h = q // per_half
            for t in range(1, chips):
                af(t, c, h).wait_recv()
                widen_chip((chip + chips - t) % chips, c, h)

        @pl.when(has_from)
        def _():
            pz(c, q).wait_recv()

        stencil(c, q)
        if q == 0:
            local_a(c).wait()
            ac(c).wait_recv()
            for h in range(HALVES):
                widen_chip(chip, c, h)
        if q == QUARTERS - 1:
            multiply(c)

    total = comps * QUARTERS
    rounds = slabs // 2 - 1 if reduce_here else 0
    assert rounds <= total
    for g in range(total):
        c, q = divmod(g, QUARTERS)
        px(c, q).wait_recv()
        if g < rounds:
            tell_near(far.at[g])

        @pl.when(has_to)
        def _():
            pz(c, q).start()

        if q % per_half == per_half - 1:
            h = q // per_half
            for t in range(1, chips):
                ay(t, c, h).wait_recv()
                af(t, c, h).start()
        if 0 <= g - LAG:
            finish(g - LAG)
        if g < rounds:
            pl.semaphore_wait(far.at[g], near)
    for g in range(total - LAG, total):
        finish(g)

    if reduce_here:
        share = cols // slabs

        def rows_of(slab):
            return pl.ds(pl.multiple_of(slab * share, share), share)

        def scatter(k):
            to = (i + k) % slabs
            return remote(acc.at[rows_of(to)], rs.at[k], rs_s.at[k], rs_r.at[k], to, n)

        def gather(k):
            return remote(rs.at[0], out_ref.at[rows_of(i)], ag_s.at[k], ag_r.at[k],
                          (i + k) % slabs, n)

        def gathered(k):
            source = (i + slabs - k) % slabs
            return remote(rs.at[0], out_ref.at[rows_of(source)], ag_s.at[k], ag_r.at[k],
                          (i + k) % slabs, n)

        for k in range(1, slabs):
            scatter(k).start()
        summed = acc[rows_of(i), :]
        for k in range(1, slabs):
            scatter(k).wait_recv()
            summed = summed + rs[k]
        summed = summed * scale
        rs[0] = summed
        for k in range(1, slabs):
            gather(k).start()
        out_ref[rows_of(i), :] = summed
        for k in range(1, slabs):
            gathered(k).wait_recv()
        for k in range(1, slabs):
            scatter(k).wait_send()
            gather(k).wait_send()
    else:
        out_ref[...] = acc[...] * scale

    for c in range(comps):
        ac(c).wait_send()
        for q in range(QUARTERS):
            px(c, q).wait_send()

            @pl.when(has_to)
            def _():
                pz(c, q).wait_send()

        for t in range(1, chips):
            for h in range(HALVES):
                ay(t, c, h).wait_send()
                af(t, c, h).wait_send()


def tiles_first(block):
    lead, (planes, cells) = block.shape[:-2], block.shape[-2:]
    split = block.reshape(lead + (planes, cells // LANES, LANES))
    return jnp.swapaxes(split, -3, -2).reshape(lead + (planes * cells // LANES, LANES))


def per_device(slabs, snaps, direct, adjoint, viscosity, energy):
    cols, comps, planes, cells = direct.shape
    rows = planes * cells // LANES
    scale = 1.0 / (8.0 * math.sqrt(comps * planes * slabs * cells))
    reduce_here = cols % (8 * slabs) == 0
    rounds = slabs // 2 - 1 if reduce_here else 0
    share = cols // slabs if reduce_here else 8
    halves = (snaps // 2, comps, HALVES)
    quarters = (comps, QUARTERS)
    dma = pltpu.SemaphoreType.DMA
    block = (cols, comps, rows, LANES)
    vmem = pl.BlockSpec(memory_space=pltpu.VMEM)
    hbm = pl.BlockSpec(memory_space=pltpu.HBM)
    out = pl.pallas_call(
        functools.partial(kernel, slabs, snaps, reduce_here, scale),
        out_shape=jax.ShapeDtypeStruct((cols, snaps * cols), jnp.float32),
        in_specs=[hbm] * 5,
        out_specs=vmem,
        scratch_shapes=[
            pltpu.VMEM((rows, LANES), jnp.float32),
            pltpu.VMEM((cells // LANES, LANES), jnp.float32),
            pltpu.VMEM((LANES, 3 * LANES), jnp.bfloat16),
            pltpu.SemaphoreType.REGULAR((max(rounds, 1),)),
            pltpu.VMEM(block, jnp.bfloat16),
            pltpu.VMEM((2,) + block, jnp.bfloat16),
            pltpu.VMEM((snaps,) + block, jnp.bfloat16),
            pltpu.VMEM((cols // HALVES * rows, LANES), jnp.float32),
            pltpu.VMEM((cols * rows, LANES), jnp.float32),
            pltpu.VMEM((snaps * cols, rows * LANES), jnp.bfloat16),
            pltpu.VMEM((cols, rows * LANES), jnp.bfloat16),
            pltpu.VMEM((rows, LANES), jnp.float32),
            pltpu.VMEM((cols, snaps * cols), jnp.float32),
            pltpu.VMEM((max(slabs, 1) if reduce_here else 1, share, snaps * cols), jnp.float32),
            dma((3, max(comps, 3))),
            dma(quarters), dma(quarters),
            dma(quarters), dma(quarters),
            dma((comps,)), dma((comps,)),
            dma(halves), dma(halves),
            dma(halves), dma(halves),
            dma((slabs,)), dma((slabs,)),
            dma((slabs,)), dma((slabs,)),
        ],
        compiler_params=pltpu.CompilerParams(collective_id=0, has_side_effects=True),
    )(
        tiles_first(direct), tiles_first(adjoint), tiles_first(viscosity),
        energy.reshape(cells // LANES, LANES), jnp.asarray(plane_matrix(), jnp.bfloat16),
    )
    if not reduce_here:
        out = lax.psum(out, "slab")
    return out.T


def solution(mesh):
    placed = (P("snap", None, "slab", None), P("snap", None, "slab", None), P("slab", None), P())
    body = functools.partial(per_device, mesh.shape["slab"], mesh.shape["snap"])
    return jax.shard_map(
        body, mesh=mesh, in_specs=placed, out_specs=P(None, "snap"), check_vma=False
    )
```

```python
import functools
import math

import jax
import jax.numpy as jnp
import numpy as np
from jax import lax
from jax.experimental import pallas as pl
from jax.experimental.pallas import tpu as pltpu
from jax.sharding import PartitionSpec as P

NY = 32
NZ = 32
LANES = 128
QUARTERS = 4
HALVES = 2
LAG = 3
GROUP = 16


def plane_matrix():
    inner = np.zeros((LANES, LANES), np.float32)
    up = np.zeros((LANES, LANES), np.float32)
    down = np.zeros((LANES, LANES), np.float32)
    for lane in range(LANES):
        row, z = divmod(lane, NZ)
        inner[lane, lane] -= 4.0
        inner[row * NZ + (z + 1) % NZ, lane] += 1.0
        inner[row * NZ + (z - 1) % NZ, lane] += 1.0
        if lane + NZ < LANES:
            inner[lane + NZ, lane] += 1.0
        else:
            down[lane + NZ - LANES, lane] += 1.0
        if lane - NZ >= 0:
            inner[lane - NZ, lane] += 1.0
        else:
            up[lane - NZ + LANES, lane] += 1.0
    return np.concatenate([inner, up, down], axis=1)


def kernel(slabs, snaps, reduce_here, scale,
           d_ref, a_ref, v_hbm, e_hbm, m_hbm, out_ref,
           v_ref, e_ref, m_ref, far, dv, halo, av, at, wt, ab, wb, e16, acc, rs,
           loc_sem, px_s, px_r, pz_s, pz_r, ac_s, ac_r, ay_s, ay_r, af_s, af_r,
           rs_s, rs_r, ag_s, ag_r):
    cols, comps, rows = d_ref.shape[0], d_ref.shape[1], d_ref.shape[2]
    chips = snaps // 2
    i = lax.axis_index("slab")
    n = lax.axis_index("snap")
    parity = i % 2
    pair = i + 1 - 2 * parity
    step = 2 - 4 * parity
    z_to = i + step
    z_from = i - step
    has_to = jnp.logical_and(z_to >= 0, z_to < slabs)
    has_from = jnp.logical_and(z_from >= 0, z_from < slabs)
    chip, core = n // 2, n % 2
    mate = chip * 2 + 1 - core
    pair_slot = 1 - parity
    z_slot = parity
    dq = cols // QUARTERS
    per_half = QUARTERS // HALVES
    ah = cols // HALVES

    def dev(slab, snap):
        return {"slab": slab, "snap": snap}

    def remote(src, dst, s, r, slab, snap):
        return pltpu.make_async_remote_copy(
            src_ref=src, dst_ref=dst, send_sem=s, recv_sem=r,
            device_id=dev(slab, snap), device_id_type=pl.DeviceIdType.MESH)

    def px(c, q):
        part = pl.ds(q * dq, dq)
        return remote(d_ref.at[part, c], halo.at[parity, part, c],
                      px_s.at[c, q], px_r.at[c, q], pair, n)

    def pz(c, q):
        part = pl.ds(q * dq, dq)
        return remote(halo.at[pair_slot, part, c], halo.at[z_slot, part, c],
                      pz_s.at[c, q], pz_r.at[c, q], z_to, n)

    def ac(c):
        return remote(a_ref.at[:, c], av.at[n, :, c], ac_s.at[c], ac_r.at[c], i, mate)

    def ay(t, c, h):
        part = pl.ds(h * ah, ah)
        return remote(a_ref.at[part, c], av.at[n, part, c],
                      ay_s.at[t, c, h], ay_r.at[t, c, h], i, ((chip + t) % chips) * 2 + core)

    def af(t, c, h):
        part = pl.ds(h * ah, ah)
        source = ((chip + chips - t) % chips) * 2 + core
        return remote(av.at[source, part, c], av.at[source, part, c],
                      af_s.at[t, c, h], af_r.at[t, c, h], i, mate)

    def local_d(c):
        return pltpu.make_async_copy(d_ref.at[:, c], dv.at[:, c], loc_sem.at[0, c])

    def local_a(c):
        return pltpu.make_async_copy(a_ref.at[:, c], av.at[n, :, c], loc_sem.at[1, c])

    barrier = pltpu.get_barrier_semaphore()

    def greet(slab, snap):
        pl.semaphore_signal(barrier, 1, device_id=dev(slab, snap),
                            device_id_type=pl.DeviceIdType.MESH)

    greet(i, mate)
    for t in range(1, chips):
        greet(i, ((chip + t) % chips) * 2 + core)
    near = 1 + has_to.astype(jnp.int32) + has_from.astype(jnp.int32)

    def tell_near(sem):
        def tell(slab):
            pl.semaphore_signal(sem, 1, device_id=dev(slab, n),
                                device_id_type=pl.DeviceIdType.MESH)

        tell(pair)
        pl.when(has_to)(lambda: tell(z_to))
        pl.when(has_from)(lambda: tell(z_from))

    tell_near(barrier)
    small = [pltpu.make_async_copy(v_hbm, v_ref, loc_sem.at[2, 0]),
             pltpu.make_async_copy(e_hbm, e_ref, loc_sem.at[2, 1]),
             pltpu.make_async_copy(m_hbm, m_ref, loc_sem.at[2, 2])]
    for copy in small:
        copy.start()
    for c in range(comps):
        local_d(c).start()
        local_a(c).start()
    pl.semaphore_wait(barrier, chips + near)

    for c in range(comps):
        for q in range(QUARTERS):
            px(c, q).start()
        for h in range(HALVES):
            for t in range(1, chips):
                ay(t, c, h).start()
    for c in range(comps):
        ac(c).start()
    for copy in small:
        copy.wait()
    for j in range(rows // 2):
        e16[2 * j:2 * j + 2, :] = jnp.broadcast_to(e_ref[j:j + 1, :], (2, LANES))

    @pl.when(jnp.logical_not(has_from))
    def _():
        halo[z_slot] = jnp.zeros(halo.shape[1:], halo.dtype)

    group = GROUP
    span = group * rows
    row_at = lax.broadcasted_iota(jnp.int32, (span, LANES), 0)
    odd = row_at % 2 == 1
    in_snap = row_at % rows

    def stencil(c, q):
        v = jnp.concatenate([v_ref[...]] * group, axis=0)
        e = jnp.concatenate([e16[...]] * group, axis=0)

        def body(g, carry):
            at_snap = q * dq + g * group
            part = pl.ds(at_snap, group)
            o16 = dv[part, c].reshape(span, LANES)
            lo = halo[0, part, c].reshape(span, LANES).astype(jnp.float32)
            hi = halo[1, part, c].reshape(span, LANES).astype(jnp.float32)
            o = o16.astype(jnp.float32)
            y = jnp.dot(o16, m_ref[...], preferred_element_type=jnp.float32)
            t = o + jnp.where(odd, lo, hi)
            swapped = jnp.where(odd, pltpu.roll(t, 1, 0), pltpu.roll(t, span - 1, 0))
            stream = (16.0 * swapped - 30.0 * o - lo - hi) * (1.0 / 12.0)
            up = pltpu.roll(y[:, LANES:2 * LANES], 2, 0)
            down = pltpu.roll(y[:, 2 * LANES:], span - 2, 0)
            lap = stream + y[:, :LANES]
            lap = lap + jnp.where(in_snap >= 2, up, 0.0)
            lap = lap + jnp.where(in_snap < rows - 2, down, 0.0)
            wt[pl.ds(pl.multiple_of(at_snap * rows, span), span), :] = e * (v * lap - o)
            return carry

        lax.fori_loop(0, dq // group, body, 0)

    def widen(b, c, h):
        first = b * cols + h * ah
        at[...] = av[b, pl.ds(h * ah, ah), c].reshape(ah * rows, LANES).astype(jnp.float32)
        for r in range(rows):
            ab[pl.ds(pl.multiple_of(first, ah), ah), r * LANES:(r + 1) * LANES] = at[
                pl.ds(r, ah, stride=rows), :].astype(jnp.bfloat16)

    def widen_chip(chip_at, c, h):
        for b in range(2):
            widen(chip_at * 2 + b, c, h)

    def multiply(c):
        for r in range(rows):
            wb[:, r * LANES:(r + 1) * LANES] = wt[
                pl.ds(r, cols, stride=rows), :].astype(jnp.bfloat16)
        tile = lax.dot_general(wb[...], ab[...], (((1,), (1,)), ((), ())),
                               preferred_element_type=jnp.float32)
        if c == 0:
            acc[...] = tile
        else:
            acc[...] += tile

    def finish(g):
        c, q = divmod(g, QUARTERS)
        if q == 0:
            local_d(c).wait()
        if q % per_half == per_half - 1:
            h = q // per_half
            for t in range(1, chips):
                af(t, c, h).wait_recv()
                widen_chip((chip + chips - t) % chips, c, h)

        @pl.when(has_from)
        def _():
            pz(c, q).wait_recv()

        stencil(c, q)
        if q == 0:
            local_a(c).wait()
            ac(c).wait_recv()
            for h in range(HALVES):
                widen_chip(chip, c, h)
        if q == QUARTERS - 1:
            multiply(c)

    total = comps * QUARTERS
    rounds = slabs // 2 - 1 if reduce_here else 0
    assert rounds <= total
    for g in range(total):
        c, q = divmod(g, QUARTERS)
        px(c, q).wait_recv()
        if g < rounds:
            tell_near(far.at[g])

        @pl.when(has_to)
        def _():
            pz(c, q).start()

        if q % per_half == per_half - 1:
            h = q // per_half
            for t in range(1, chips):
                ay(t, c, h).wait_recv()
                af(t, c, h).start()
        if 0 <= g - LAG:
            finish(g - LAG)
        if g < rounds:
            pl.semaphore_wait(far.at[g], near)
    for g in range(total - LAG, total):
        finish(g)

    if reduce_here:
        share = cols // slabs

        def rows_of(slab):
            return pl.ds(pl.multiple_of(slab * share, share), share)

        def scatter(k):
            to = (i + k) % slabs
            return remote(acc.at[rows_of(to)], rs.at[k], rs_s.at[k], rs_r.at[k], to, n)

        def gather(k):
            return remote(rs.at[0], out_ref.at[rows_of(i)], ag_s.at[k], ag_r.at[k],
                          (i + k) % slabs, n)

        def gathered(k):
            source = (i + slabs - k) % slabs
            return remote(rs.at[0], out_ref.at[rows_of(source)], ag_s.at[k], ag_r.at[k],
                          (i + k) % slabs, n)

        for k in range(1, slabs):
            scatter(k).start()
        summed = acc[rows_of(i), :]
        for k in range(1, slabs):
            scatter(k).wait_recv()
            summed = summed + rs[k]
        summed = summed * scale
        rs[0] = summed
        for k in range(1, slabs):
            gather(k).start()
        own = pltpu.make_async_copy(rs.at[0], out_ref.at[rows_of(i)], loc_sem.at[0, 0])
        own.start()
        for k in range(1, slabs):
            gathered(k).wait_recv()
        own.wait()
        for k in range(1, slabs):
            scatter(k).wait_send()
            gather(k).wait_send()
    else:
        acc[...] = acc[...] * scale
        whole = pltpu.make_async_copy(acc, out_ref, loc_sem.at[0, 0])
        whole.start()
        whole.wait()

    for c in range(comps):
        ac(c).wait_send()
        for q in range(QUARTERS):
            px(c, q).wait_send()

            @pl.when(has_to)
            def _():
                pz(c, q).wait_send()

        for t in range(1, chips):
            for h in range(HALVES):
                ay(t, c, h).wait_send()
                af(t, c, h).wait_send()


def tiles_first(block):
    lead, (planes, cells) = block.shape[:-2], block.shape[-2:]
    split = block.reshape(lead + (planes, cells // LANES, LANES))
    return jnp.swapaxes(split, -3, -2).reshape(lead + (planes * cells // LANES, LANES))


def per_device(slabs, snaps, direct, adjoint, viscosity, energy):
    cols, comps, planes, cells = direct.shape
    rows = planes * cells // LANES
    scale = 1.0 / (8.0 * math.sqrt(comps * planes * slabs * cells))
    reduce_here = cols % (8 * slabs) == 0
    rounds = slabs // 2 - 1 if reduce_here else 0
    share = cols // slabs if reduce_here else 8
    halves = (snaps // 2, comps, HALVES)
    quarters = (comps, QUARTERS)
    dma = pltpu.SemaphoreType.DMA
    block = (cols, comps, rows, LANES)
    hbm = pl.BlockSpec(memory_space=pltpu.HBM)
    out = pl.pallas_call(
        functools.partial(kernel, slabs, snaps, reduce_here, scale),
        out_shape=jax.ShapeDtypeStruct((cols, snaps * cols), jnp.float32),
        in_specs=[hbm] * 5,
        out_specs=hbm,
        scratch_shapes=[
            pltpu.VMEM((rows, LANES), jnp.float32),
            pltpu.VMEM((cells // LANES, LANES), jnp.float32),
            pltpu.VMEM((LANES, 3 * LANES), jnp.bfloat16),
            pltpu.SemaphoreType.REGULAR((max(rounds, 1),)),
            pltpu.VMEM(block, jnp.bfloat16),
            pltpu.VMEM((2,) + block, jnp.bfloat16),
            pltpu.VMEM((snaps,) + block, jnp.bfloat16),
            pltpu.VMEM((cols // HALVES * rows, LANES), jnp.float32),
            pltpu.VMEM((cols * rows, LANES), jnp.float32),
            pltpu.VMEM((snaps * cols, rows * LANES), jnp.bfloat16),
            pltpu.VMEM((cols, rows * LANES), jnp.bfloat16),
            pltpu.VMEM((rows, LANES), jnp.float32),
            pltpu.VMEM((cols, snaps * cols), jnp.float32),
            pltpu.VMEM((max(slabs, 1) if reduce_here else 1, share, snaps * cols), jnp.float32),
            dma((3, max(comps, 3))),
            dma(quarters), dma(quarters),
            dma(quarters), dma(quarters),
            dma((comps,)), dma((comps,)),
            dma(halves), dma(halves),
            dma(halves), dma(halves),
            dma((slabs,)), dma((slabs,)),
            dma((slabs,)), dma((slabs,)),
        ],
        compiler_params=pltpu.CompilerParams(collective_id=0, has_side_effects=True),
    )(
        tiles_first(direct), tiles_first(adjoint), tiles_first(viscosity),
        energy.reshape(cells // LANES, LANES), jnp.asarray(plane_matrix(), jnp.bfloat16),
    )
    if not reduce_here:
        out = lax.psum(out, "slab")
    return out.T


def solution(mesh):
    placed = (P("snap", None, "slab", None), P("snap", None, "slab", None), P("slab", None), P())
    body = functools.partial(per_device, mesh.shape["slab"], mesh.shape["snap"])
    return jax.shard_map(
        body, mesh=mesh, in_specs=placed, out_specs=P(None, "snap"), check_vma=False
    )
```

```python
import functools
import math

import jax
import jax.numpy as jnp
import numpy as np
from jax import lax
from jax.experimental import pallas as pl
from jax.experimental.pallas import tpu as pltpu
from jax.sharding import PartitionSpec as P

NY = 32
NZ = 32
LANES = 128
QUARTERS = 4
HALVES = 2
LAG = 4
GROUP = 16


def plane_matrix():
    inner = np.zeros((LANES, LANES), np.float32)
    up = np.zeros((LANES, LANES), np.float32)
    down = np.zeros((LANES, LANES), np.float32)
    for lane in range(LANES):
        row, z = divmod(lane, NZ)
        inner[lane, lane] -= 4.0
        inner[row * NZ + (z + 1) % NZ, lane] += 1.0
        inner[row * NZ + (z - 1) % NZ, lane] += 1.0
        if lane + NZ < LANES:
            inner[lane + NZ, lane] += 1.0
        else:
            down[lane + NZ - LANES, lane] += 1.0
        if lane - NZ >= 0:
            inner[lane - NZ, lane] += 1.0
        else:
            up[lane - NZ + LANES, lane] += 1.0
    return np.concatenate([inner, up, down], axis=1)


def kernel(slabs, snaps, reduce_here, scale,
           d_ref, a_ref, v_hbm, e_hbm, m_hbm, out_ref,
           v_ref, e_ref, m_ref, far, dv, halo, av, at, wt, ab, wb, e16, acc, rs,
           loc_sem, px_s, px_r, pz_s, pz_r, ac_s, ac_r, ay_s, ay_r, af_s, af_r,
           rs_s, rs_r, ag_s, ag_r):
    cols, comps, rows = d_ref.shape[0], d_ref.shape[1], d_ref.shape[2]
    chips = snaps // 2
    i = lax.axis_index("slab")
    n = lax.axis_index("snap")
    parity = i % 2
    pair = i + 1 - 2 * parity
    step = 2 - 4 * parity
    z_to = i + step
    z_from = i - step
    has_to = jnp.logical_and(z_to >= 0, z_to < slabs)
    has_from = jnp.logical_and(z_from >= 0, z_from < slabs)
    chip, core = n // 2, n % 2
    mate = chip * 2 + 1 - core
    pair_slot = 1 - parity
    z_slot = parity
    dq = cols // QUARTERS
    per_half = QUARTERS // HALVES
    ah = cols // HALVES

    def dev(slab, snap):
        return {"slab": slab, "snap": snap}

    def remote(src, dst, s, r, slab, snap):
        return pltpu.make_async_remote_copy(
            src_ref=src, dst_ref=dst, send_sem=s, recv_sem=r,
            device_id=dev(slab, snap), device_id_type=pl.DeviceIdType.MESH)

    def px(c, q):
        part = pl.ds(q * dq, dq)
        return remote(d_ref.at[part, c], halo.at[parity, part, c],
                      px_s.at[c, q], px_r.at[c, q], pair, n)

    def pz(c, q):
        part = pl.ds(q * dq, dq)
        return remote(halo.at[pair_slot, part, c], halo.at[z_slot, part, c],
                      pz_s.at[c, q], pz_r.at[c, q], z_to, n)

    def ac(c):
        return remote(a_ref.at[:, c], av.at[n, :, c], ac_s.at[c], ac_r.at[c], i, mate)

    def ay(t, c, h):
        part = pl.ds(h * ah, ah)
        return remote(a_ref.at[part, c], av.at[n, part, c],
                      ay_s.at[t, c, h], ay_r.at[t, c, h], i, ((chip + t) % chips) * 2 + core)

    def af(t, c, h):
        part = pl.ds(h * ah, ah)
        source = ((chip + chips - t) % chips) * 2 + core
        return remote(av.at[source, part, c], av.at[source, part, c],
                      af_s.at[t, c, h], af_r.at[t, c, h], i, mate)

    def local_d(c):
        return pltpu.make_async_copy(d_ref.at[:, c], dv.at[:, c], loc_sem.at[0, c])

    def local_a(c):
        return pltpu.make_async_copy(a_ref.at[:, c], av.at[n, :, c], loc_sem.at[1, c])

    barrier = pltpu.get_barrier_semaphore()

    def greet(slab, snap):
        pl.semaphore_signal(barrier, 1, device_id=dev(slab, snap),
                            device_id_type=pl.DeviceIdType.MESH)

    greet(i, mate)
    for t in range(1, chips):
        greet(i, ((chip + t) % chips) * 2 + core)
    near = 1 + has_to.astype(jnp.int32) + has_from.astype(jnp.int32)

    def tell_near(sem):
        def tell(slab):
            pl.semaphore_signal(sem, 1, device_id=dev(slab, n),
                                device_id_type=pl.DeviceIdType.MESH)

        tell(pair)
        pl.when(has_to)(lambda: tell(z_to))
        pl.when(has_from)(lambda: tell(z_from))

    tell_near(barrier)
    small = [pltpu.make_async_copy(v_hbm, v_ref, loc_sem.at[2, 0]),
             pltpu.make_async_copy(e_hbm, e_ref, loc_sem.at[2, 1]),
             pltpu.make_async_copy(m_hbm, m_ref, loc_sem.at[2, 2])]
    for copy in small:
        copy.start()
    for c in range(comps):
        local_d(c).start()
        local_a(c).start()
    pl.semaphore_wait(barrier, chips + near)

    for c in range(comps):
        for q in range(QUARTERS):
            px(c, q).start()
        for h in range(HALVES):
            for t in range(1, chips):
                ay(t, c, h).start()
    for c in range(comps):
        ac(c).start()
    for copy in small:
        copy.wait()
    for j in range(rows // 2):
        e16[2 * j:2 * j + 2, :] = jnp.broadcast_to(e_ref[j:j + 1, :], (2, LANES))

    @pl.when(jnp.logical_not(has_from))
    def _():
        halo[z_slot] = jnp.zeros(halo.shape[1:], halo.dtype)

    group = GROUP
    span = group * rows
    row_at = lax.broadcasted_iota(jnp.int32, (span, LANES), 0)
    odd = row_at % 2 == 1
    in_snap = row_at % rows

    def stencil(c, q):
        v = jnp.concatenate([v_ref[...]] * group, axis=0)
        e = jnp.concatenate([e16[...]] * group, axis=0)

        def body(g, carry):
            at_snap = q * dq + g * group
            part = pl.ds(at_snap, group)
            o16 = dv[part, c].reshape(span, LANES)
            lo = halo[0, part, c].reshape(span, LANES).astype(jnp.float32)
            hi = halo[1, part, c].reshape(span, LANES).astype(jnp.float32)
            o = o16.astype(jnp.float32)
            y = jnp.dot(o16, m_ref[...], preferred_element_type=jnp.float32)
            t = o + jnp.where(odd, lo, hi)
            swapped = jnp.where(odd, pltpu.roll(t, 1, 0), pltpu.roll(t, span - 1, 0))
            stream = (16.0 * swapped - 30.0 * o - lo - hi) * (1.0 / 12.0)
            up = pltpu.roll(y[:, LANES:2 * LANES], 2, 0)
            down = pltpu.roll(y[:, 2 * LANES:], span - 2, 0)
            lap = stream + y[:, :LANES]
            lap = lap + jnp.where(in_snap >= 2, up, 0.0)
            lap = lap + jnp.where(in_snap < rows - 2, down, 0.0)
            wt[pl.ds(pl.multiple_of(at_snap * rows, span), span), :] = e * (v * lap - o)
            return carry

        lax.fori_loop(0, dq // group, body, 0)

    def widen(b, c, h):
        first = b * cols + h * ah
        at[...] = av[b, pl.ds(h * ah, ah), c].reshape(ah * rows, LANES).astype(jnp.float32)
        for r in range(rows):
            ab[pl.ds(pl.multiple_of(first, ah), ah), r * LANES:(r + 1) * LANES] = at[
                pl.ds(r, ah, stride=rows), :].astype(jnp.bfloat16)

    def widen_chip(chip_at, c, h):
        for b in range(2):
            widen(chip_at * 2 + b, c, h)

    def multiply(c):
        for r in range(rows):
            wb[:, r * LANES:(r + 1) * LANES] = wt[
                pl.ds(r, cols, stride=rows), :].astype(jnp.bfloat16)
        tile = lax.dot_general(wb[...], ab[...], (((1,), (1,)), ((), ())),
                               preferred_element_type=jnp.float32)
        if c == 0:
            acc[...] = tile
        else:
            acc[...] += tile

    def finish(g):
        c, q = divmod(g, QUARTERS)
        if q == 0:
            local_d(c).wait()
        if q % per_half == per_half - 1:
            h = q // per_half
            for t in range(1, chips):
                af(t, c, h).wait_recv()
                widen_chip((chip + chips - t) % chips, c, h)

        @pl.when(has_from)
        def _():
            pz(c, q).wait_recv()

        stencil(c, q)
        if q == 0:
            local_a(c).wait()
            ac(c).wait_recv()
            for h in range(HALVES):
                widen_chip(chip, c, h)
        if q == QUARTERS - 1:
            multiply(c)

    total = comps * QUARTERS
    rounds = slabs // 2 - 1 if reduce_here else 0
    assert rounds <= total
    for g in range(total):
        c, q = divmod(g, QUARTERS)
        px(c, q).wait_recv()
        if g < rounds:
            tell_near(far.at[g])

        @pl.when(has_to)
        def _():
            pz(c, q).start()

        if q % per_half == per_half - 1:
            h = q // per_half
            for t in range(1, chips):
                ay(t, c, h).wait_recv()
                af(t, c, h).start()
        if 0 <= g - LAG:
            finish(g - LAG)
        if g < rounds:
            pl.semaphore_wait(far.at[g], near)
    for g in range(total - LAG, total):
        finish(g)

    if reduce_here:
        share = cols // slabs

        def rows_of(slab):
            return pl.ds(pl.multiple_of(slab * share, share), share)

        def scatter(k):
            to = (i + k) % slabs
            return remote(acc.at[rows_of(to)], rs.at[k], rs_s.at[k], rs_r.at[k], to, n)

        def gather(k):
            return remote(rs.at[0], out_ref.at[rows_of(i)], ag_s.at[k], ag_r.at[k],
                          (i + k) % slabs, n)

        def gathered(k):
            source = (i + slabs - k) % slabs
            return remote(rs.at[0], out_ref.at[rows_of(source)], ag_s.at[k], ag_r.at[k],
                          (i + k) % slabs, n)

        for k in range(1, slabs):
            scatter(k).start()
        summed = acc[rows_of(i), :]
        for k in range(1, slabs):
            scatter(k).wait_recv()
            summed = summed + rs[k]
        summed = summed * scale
        rs[0] = summed
        for k in range(1, slabs):
            gather(k).start()
        own = pltpu.make_async_copy(rs.at[0], out_ref.at[rows_of(i)], loc_sem.at[0, 0])
        own.start()
        for k in range(1, slabs):
            gathered(k).wait_recv()
        own.wait()
        for k in range(1, slabs):
            scatter(k).wait_send()
            gather(k).wait_send()
    else:
        acc[...] = acc[...] * scale
        whole = pltpu.make_async_copy(acc, out_ref, loc_sem.at[0, 0])
        whole.start()
        whole.wait()

    for c in range(comps):
        ac(c).wait_send()
        for q in range(QUARTERS):
            px(c, q).wait_send()

            @pl.when(has_to)
            def _():
                pz(c, q).wait_send()

        for t in range(1, chips):
            for h in range(HALVES):
                ay(t, c, h).wait_send()
                af(t, c, h).wait_send()


def tiles_first(block):
    lead, (planes, cells) = block.shape[:-2], block.shape[-2:]
    split = block.reshape(lead + (planes, cells // LANES, LANES))
    return jnp.swapaxes(split, -3, -2).reshape(lead + (planes * cells // LANES, LANES))


def per_device(slabs, snaps, direct, adjoint, viscosity, energy):
    cols, comps, planes, cells = direct.shape
    rows = planes * cells // LANES
    scale = 1.0 / (8.0 * math.sqrt(comps * planes * slabs * cells))
    reduce_here = cols % (8 * slabs) == 0
    rounds = slabs // 2 - 1 if reduce_here else 0
    share = cols // slabs if reduce_here else 8
    halves = (snaps // 2, comps, HALVES)
    quarters = (comps, QUARTERS)
    dma = pltpu.SemaphoreType.DMA
    block = (cols, comps, rows, LANES)
    hbm = pl.BlockSpec(memory_space=pltpu.HBM)
    out = pl.pallas_call(
        functools.partial(kernel, slabs, snaps, reduce_here, scale),
        out_shape=jax.ShapeDtypeStruct((cols, snaps * cols), jnp.float32),
        in_specs=[hbm] * 5,
        out_specs=hbm,
        scratch_shapes=[
            pltpu.VMEM((rows, LANES), jnp.float32),
            pltpu.VMEM((cells // LANES, LANES), jnp.float32),
            pltpu.VMEM((LANES, 3 * LANES), jnp.bfloat16),
            pltpu.SemaphoreType.REGULAR((max(rounds, 1),)),
            pltpu.VMEM(block, jnp.bfloat16),
            pltpu.VMEM((2,) + block, jnp.bfloat16),
            pltpu.VMEM((snaps,) + block, jnp.bfloat16),
            pltpu.VMEM((cols // HALVES * rows, LANES), jnp.float32),
            pltpu.VMEM((cols * rows, LANES), jnp.float32),
            pltpu.VMEM((snaps * cols, rows * LANES), jnp.bfloat16),
            pltpu.VMEM((cols, rows * LANES), jnp.bfloat16),
            pltpu.VMEM((rows, LANES), jnp.float32),
            pltpu.VMEM((cols, snaps * cols), jnp.float32),
            pltpu.VMEM((max(slabs, 1) if reduce_here else 1, share, snaps * cols), jnp.float32),
            dma((3, max(comps, 3))),
            dma(quarters), dma(quarters),
            dma(quarters), dma(quarters),
            dma((comps,)), dma((comps,)),
            dma(halves), dma(halves),
            dma(halves), dma(halves),
            dma((slabs,)), dma((slabs,)),
            dma((slabs,)), dma((slabs,)),
        ],
        compiler_params=pltpu.CompilerParams(collective_id=0, has_side_effects=True),
    )(
        tiles_first(direct), tiles_first(adjoint), tiles_first(viscosity),
        energy.reshape(cells // LANES, LANES), jnp.asarray(plane_matrix(), jnp.bfloat16),
    )
    if not reduce_here:
        out = lax.psum(out, "slab")
    return out.T


def solution(mesh):
    placed = (P("snap", None, "slab", None), P("snap", None, "slab", None), P("slab", None), P())
    body = functools.partial(per_device, mesh.shape["slab"], mesh.shape["snap"])
    return jax.shard_map(
        body, mesh=mesh, in_specs=placed, out_specs=P(None, "snap"), check_vma=False
    )
```
